32 devices in a mesh: ctx: 4 (over y, x), vis: 8 (over z, core).
Axes of the slice: x: 2, y: 2, z: 4, core: 2. Of those that a mesh axis runs over, the one named last changes fastest.
Arguments:
- patches: bfloat16 [4096, 1280], P(('ctx', 'vis')), may hold values from -10 to 10
- vis_gain: float32 [1280], replicated, may hold values from 0.5 to 1.5
- w_qkv: bfloat16 [1280, 3840], P(None, 'vis'), may hold values from -2 to 2
- w_out: bfloat16 [1280, 1280], P('vis'), may hold values from -0.15625 to 0.15625
- merge_gain: float32 [1280], replicated, may hold values from 0.5 to 1.5
- w_merge: bfloat16 [5120, 8192], P(None, 'vis'), may hold values from -0.078125 to 0.078125
- token_dest: int32 [4, 256], replicated, may hold values from 0 to 3, as said below
- token_row: int32 [4, 256], replicated, may hold values from 0 to 1023, as said below
- prompt_text: bfloat16 [4096, 8192], P('ctx', 'vis'), may hold values from -6 to 6
- kv_gain: float32 [8192], P('vis'), may hold values from 0.5 to 1.5
- w_kv: bfloat16 [8192, 1024], P('vis'), may hold values from -1 to 1
- queries: bfloat16 [512, 4096], P('ctx'), may hold values from -12 to 12
- resp_kv: bfloat16 [512, 1024], P('ctx'), may hold values from -12 to 12
- resp_len: int32 [4], P('ctx'), may hold values from 64 to 128
Outputs:
- attended: bfloat16 [512, 4096], P('ctx')
The draws below stay inside these ranges and needn't reach their ends.
Inputs may be any that keep to these rules, and one draw needn't show every extreme that they name: `token_dest`: the tokens of one image are in order of their prompt shard; at most 96 tokens of one image go to one shard, and from every image exactly 96 go to some shard. `token_row`: no two visual tokens take the same position of one shard.
All inputs are finite; a program needn't handle non-finite values.
Results may differ from the reference program's by a relative error of at most 0.014.
Values may be sent and summed in bfloat16 or wider, within the bound.
A program may use at most 128 MiB of HBM per device.

```python
import math
import jax
import jax.numpy as jnp
from jax import lax

VD = 1280
VHEADS = 16
D = 8192
HD = 128
QH = 32
KVH = 4
CROWS = 1024
R_TOK = 128
VHD = 80
MD = 5120
GP = 1024
VTOK = 256
IMAGES = 4
BASE = 64
L = 4096
RESP = 512
N_CTX = 4


def routing_tables(key):
    count = IMAGES
    half = BASE // 2
    spare = jax.random.randint(jax.random.fold_in(key, 11), (count, count), 0, half + 1)
    diagonal = jnp.arange(count)
    spare = spare.at[diagonal, diagonal].set(half)
    spare = spare.at[diagonal, (diagonal + 1) % count].set(0)
    amounts = BASE + spare - jnp.roll(spare, -1, axis=1)
    running = jnp.cumsum(amounts, axis=1)
    tokens = jnp.arange(VTOK)
    dest = jnp.sum((tokens[None, :, None] >= running[:, None, :]).astype(jnp.int32), axis=2)
    row_first = running - amounts
    within = tokens[None, :] - jnp.take_along_axis(row_first, dest, axis=1)
    column_first = jnp.cumsum(amounts, axis=0) - amounts
    offset = jnp.take_along_axis(column_first, dest, axis=1)
    keys = jax.random.split(jax.random.fold_in(key, 12), count)
    orders = jax.vmap(lambda single: jax.random.permutation(single, CROWS))(keys)
    rows = orders[dest, offset + within]
    return (dest.astype(jnp.int32), rows.astype(jnp.int32))


def draw_token_dest(key, part):
    return routing_tables(key)[0]


def draw_token_row(key, part):
    return routing_tables(key)[1]


def draw_patches(key, part):
    shape = (N_CTX * GP, VD)
    noise_key = jax.random.fold_in(key, 41)
    base = jax.random.truncated_normal(noise_key, -6.0, 6.0, shape, jnp.float32)
    return base.astype(jnp.bfloat16)


def draw_w_qkv(key, part):
    base = jax.random.truncated_normal(jax.random.fold_in(key, 51), -6.0, 6.0, (VD, 3 * VD), jnp.float32)
    base = base / math.sqrt(VD)
    return base.astype(jnp.bfloat16)


def draw_prompt_text(key, part):
    shape = (L, D)
    noise_key = jax.random.fold_in(key, 81)
    base = jax.random.truncated_normal(noise_key, -6.0, 6.0, shape, jnp.float32)
    return base.astype(jnp.bfloat16)


def draw_w_kv(key, part):
    width = KVH * HD
    base = jax.random.truncated_normal(jax.random.fold_in(key, 91), -6.0, 6.0, (D, 2 * width), jnp.float32)
    base = base / math.sqrt(D)
    return base.astype(jnp.bfloat16)


def draw_resp_kv(key, part):
    shape = (RESP, 2 * KVH * HD)
    noise_key = jax.random.fold_in(key, 61)
    base = jax.random.truncated_normal(noise_key, -6.0, 6.0, shape, jnp.float32)
    return base.astype(jnp.bfloat16)


def draw_queries(key, part):
    shape = (RESP, QH * HD)
    noise_key = jax.random.fold_in(key, 71)
    base = 3.0 * jax.random.truncated_normal(noise_key, -4.0, 4.0, shape, jnp.float32)
    return base.astype(jnp.bfloat16)


def set_ends(values, own_key, smallest, high):
    shape = values.shape
    place = [jax.random.randint(jax.random.fold_in(own_key, axis), (), 0, shape[axis]) for axis in range(len(shape))]
    values = values.at[tuple(place)].set(smallest)
    longest = shape.index(max(shape))
    place[longest] = (place[longest] + 1) % shape[longest]
    return values.at[tuple(place)].set(high)


def block_scale(stream_key, extent, cuts, smallest, largest):
    loudness, own = 1.0, jax.random.fold_in(stream_key, 6)
    for dim, shards_of in cuts:
        heights = jnp.exp(jax.random.uniform(jax.random.fold_in(own, dim), (shards_of,), jnp.float32, smallest / len(cuts), largest / len(cuts)))
        loudness = loudness * jnp.repeat(heights, extent[dim] // shards_of).reshape([-1 if axis == dim else 1 for axis in range(len(extent))])
    return loudness


def bell_draw(rng, dims, deviation, bound, cuts=(), held_as=jnp.bfloat16):
    entries = jax.random.normal(rng, dims, jnp.float32) * deviation
    if len(cuts) > 0:
        entries = block_scale(rng, dims, cuts, -0.22, 0.18) * entries
    return jnp.clip(entries, min=-bound, max=bound).astype(held_as)


def setup_inputs(seed: int = 0) -> dict:
    key_list = jax.random.split(jax.random.key(seed), 15)
    patches = draw_patches(jax.random.fold_in(key_list[14], 71), 0)
    vis_gain = jnp.clip(1.0 + 0.1 * jax.random.normal(key_list[1], (VD,), jnp.float32), 0.5, 1.5)
    w_qkv = draw_w_qkv(jax.random.fold_in(key_list[14], 71), 0)
    w_out = bell_draw(key_list[3], (VD, VD), VD ** -0.5, 0.15625, ((0, 8),))
    merge_gain = jnp.clip(1.0 + 0.1 * jax.random.normal(key_list[4], (VD,), jnp.float32), 0.5, 1.5)
    w_merge = bell_draw(key_list[5], (MD, D), MD ** -0.5, 0.078125, ((1, 8),))
    token_dest = draw_token_dest(jax.random.fold_in(key_list[14], 71), 0)
    token_row = draw_token_row(jax.random.fold_in(key_list[14], 71), 0)
    prompt_text = draw_prompt_text(jax.random.fold_in(key_list[14], 71), 0)
    kv_gain = jnp.clip(1.0 + 0.1 * jax.random.normal(key_list[9], (D,), jnp.float32), 0.5, 1.5)
    w_kv = draw_w_kv(jax.random.fold_in(key_list[14], 71), 0)
    queries = draw_queries(jax.random.fold_in(key_list[14], 71), 0)
    resp_kv = draw_resp_kv(jax.random.fold_in(key_list[14], 71), 0)
    resp_len = set_ends(jax.random.randint(key_list[13], (N_CTX,), R_TOK // 2, R_TOK + 1), jax.random.fold_in(key_list[13], 1), R_TOK // 2, R_TOK).astype(jnp.int32)
    return {"patches": patches, "vis_gain": vis_gain, "w_qkv": w_qkv, "w_out": w_out, "merge_gain": merge_gain, "w_merge": w_merge, "token_dest": token_dest, "token_row": token_row, "prompt_text": prompt_text, "kv_gain": kv_gain, "w_kv": w_kv, "queries": queries, "resp_kv": resp_kv, "resp_len": resp_len}


EPS = 1e-06

def layer_norm(values, gain):
    center = values - lax.optimization_barrier(jnp.mean(values, axis=-1, keepdims=True))
    spread = lax.optimization_barrier(jnp.mean(center * center, axis=-1, keepdims=True))
    return center * lax.rsqrt(spread + EPS) * gain.astype(jnp.float32)

def dense_attention(query, keys, values):
    count = query.shape[0]
    block = min(512, count)
    scale = 1.0 / math.sqrt(query.shape[1])

    def one_block(part):
        scores = jnp.dot(part, keys.T, preferred_element_type=jnp.float32) * scale
        highest = lax.optimization_barrier(jnp.max(scores, axis=1, keepdims=True))
        expo = jnp.exp(scores - highest)
        summed = lax.optimization_barrier(jnp.sum(expo, axis=1, keepdims=True))
        mixed = jnp.dot(expo.astype(jnp.bfloat16), values, preferred_element_type=jnp.float32)
        return (mixed / summed).astype(jnp.bfloat16)
    blocks = query.reshape(count // block, block, query.shape[1])
    return lax.map(one_block, blocks).reshape(count, values.shape[1])

def head_attention(packed):
    stacked = jnp.transpose(packed, (1, 0, 2))

    def one_head(item):
        return dense_attention(item[:, :VHD], item[:, VHD:2 * VHD], item[:, 2 * VHD:])
    return jnp.transpose(lax.map(one_head, stacked), (1, 0, 2))

def reference(patches, vis_gain, w_qkv, w_out, merge_gain, w_merge, token_dest, token_row, prompt_text, kv_gain, w_kv, queries, resp_kv, resp_len):

    def vision_image(patch_rows):
        floats = patch_rows.astype(jnp.float32)
        normed = layer_norm(floats, vis_gain).astype(jnp.bfloat16)
        qkv = jnp.dot(normed, w_qkv, preferred_element_type=jnp.float32).astype(jnp.bfloat16)
        heads = head_attention(qkv.reshape(GP, VHEADS, 3 * VHD)).reshape(GP, VD)
        mixed = floats + jnp.dot(heads, w_out, preferred_element_type=jnp.float32)
        merged = layer_norm(mixed, merge_gain).astype(jnp.bfloat16).reshape(VTOK, MD)
        return jnp.dot(merged, w_merge, preferred_element_type=jnp.float32).astype(jnp.bfloat16)
    visual = lax.map(vision_image, patches.reshape(IMAGES, GP, VD))
    places = (token_dest * CROWS + token_row).reshape(-1).astype(jnp.int32)
    prompt = prompt_text.at[places].set(visual.reshape(IMAGES * VTOK, D))

    def project_block(rows):
        floats = rows.astype(jnp.float32)
        inverse = lax.rsqrt(lax.optimization_barrier(jnp.mean(floats * floats, axis=1, keepdims=True)) + EPS)
        normed = (floats * inverse * kv_gain.astype(jnp.float32)).astype(jnp.bfloat16)
        return jnp.dot(normed, w_kv, preferred_element_type=jnp.float32).astype(jnp.bfloat16)
    kv = lax.map(project_block, prompt.reshape(N_CTX, CROWS, D)).reshape(L, 2 * KVH * HD)
    width = KVH * HD
    prompt_keys = kv[:, :width].reshape(L, KVH, HD)
    prompt_values = kv[:, width:].reshape(L, KVH, HD)
    group = QH // KVH
    scale = 1.0 / math.sqrt(HD)
    position = jnp.arange(R_TOK, dtype=jnp.int32)
    visible = jnp.concatenate([jnp.ones((R_TOK, L), dtype=bool), position[None, :] <= position[:, None]], axis=1)

    def one_response(items):
        query, own, length = items
        q_heads = jnp.transpose(query.reshape(R_TOK, KVH, group, HD), (1, 0, 2, 3))
        keys = jnp.concatenate([prompt_keys, own[:, :width].reshape(R_TOK, KVH, HD)], axis=0)
        values = jnp.concatenate([prompt_values, own[:, width:].reshape(R_TOK, KVH, HD)], axis=0)
        keys = jnp.transpose(keys, (1, 0, 2))
        values = jnp.transpose(values, (1, 0, 2))

        def one_head(triple):
            q_part, k_part, v_part = triple
            scores = jnp.einsum('rgd,nd->grn', q_part.astype(jnp.float32), k_part.astype(jnp.float32)) * scale
            scores = jnp.where(visible[None], scores, -1e+30)
            highest = lax.optimization_barrier(jnp.max(scores, axis=2, keepdims=True))
            expo = jnp.where(visible[None], jnp.exp(scores - highest), 0.0)
            summed = lax.optimization_barrier(jnp.sum(expo, axis=2, keepdims=True))
            mixed = jnp.einsum('grn,nd->grd', expo.astype(jnp.bfloat16).astype(jnp.float32), v_part.astype(jnp.float32))
            return mixed / summed
        result = lax.map(one_head, (q_heads, keys, values))
        result = jnp.transpose(result, (2, 0, 1, 3)).reshape(R_TOK, QH * HD)
        live = (position < length)[:, None]
        return jnp.where(live, result, 0.0).astype(jnp.bfloat16)
    attended = lax.map(one_response, (queries.reshape(N_CTX, R_TOK, QH * HD), resp_kv.reshape(N_CTX, R_TOK, 2 * width), resp_len))
    return attended.reshape(RESP, QH * HD)
```

```python
import math

import jax
import jax.numpy as jnp
from jax import lax
from jax.sharding import Mesh, PartitionSpec as P

VD = 1280
VHEADS = 16
D = 8192
HD = 128
QH = 32
KVH = 4
VHD = 80
MD = 5120


EPS = 1e-06
VIS = ("vk", "vg")
F32 = jnp.float32
BF16 = jnp.bfloat16


def layer_norm(values, gain):
    center = values - jnp.mean(values, axis=-1, keepdims=True)
    spread = jnp.mean(center * center, axis=-1, keepdims=True)
    return center * lax.rsqrt(spread + EPS) * gain


def vision_attention(qkv, local_heads):
    scale = 1.0 / math.sqrt(VHD)
    outs = []
    for h in range(local_heads):
        base = h * 3 * VHD
        query = qkv[:, base : base + VHD]
        keys = qkv[:, base + VHD : base + 2 * VHD]
        values = qkv[:, base + 2 * VHD : base + 3 * VHD]
        scores = jnp.einsum("qd,kd->qk", query, keys, preferred_element_type=F32) * scale
        expo = jnp.exp(scores - jnp.max(scores, axis=1, keepdims=True))
        summed = jnp.sum(expo, axis=1, keepdims=True)
        mixed = jnp.dot(expo.astype(BF16), values, preferred_element_type=F32)
        outs.append((mixed / summed).astype(BF16))
    return jnp.concatenate(outs, axis=1)


def partial_kv(rows, weight, heads, parts):
    count = rows.shape[0]
    raw = jnp.dot(rows, weight, preferred_element_type=F32)
    floats = rows.astype(F32)
    squares = jnp.sum(floats * floats, axis=1)
    each = count // parts
    pieces = raw.reshape(parts, each, 2, heads, HD).transpose(3, 0, 1, 2, 4)
    pieces = pieces.reshape(heads * parts, each, 2 * HD)
    extra = squares.reshape(parts, each // HD // 2 if each >= 2 * HD else 1, -1)
    extra = jnp.pad(extra, ((0, 0), (0, 8 - extra.shape[1]), (0, 2 * HD - extra.shape[2])))
    extra = jnp.broadcast_to(extra[None], (heads,) + extra.shape).reshape(heads * parts, 8, 2 * HD)
    return jnp.concatenate([pieces, extra], axis=1)


def whole_kv(partial, count):
    total = lax.psum_scatter(partial, VIS, scatter_dimension=0, tiled=True)[0]
    each = total.shape[0] - 8
    rows = each // HD // 2 if each >= 2 * HD else 1
    squares = total[each : each + rows, : each // rows].reshape(each)
    inverse = lax.rsqrt(squares / D + EPS)
    share = (total[:each] * inverse[:, None]).astype(BF16)
    return lax.all_gather(share, ("ctx", "vg"), axis=0, tiled=True)


def per_device(
    patches,
    vis_gain,
    w_qkv,
    w_out,
    merge_gain,
    w_merge,
    token_dest,
    token_row,
    prompt_text,
    kv_gain,
    w_kv,
    queries,
    resp_kv,
    resp_len,
):
    vis_count = lax.axis_size("vk") * lax.axis_size("vg")
    parts = lax.axis_size("vg")
    ctx_count = lax.axis_size("ctx")
    vis_index = lax.axis_index("vk") * parts + lax.axis_index("vg")
    patch_count = patches.shape[0]
    shard_rows = prompt_text.shape[0]
    local_heads = VHEADS // vis_count

    floats = patches.astype(F32)
    normed = layer_norm(floats, vis_gain).astype(BF16)
    gathered = lax.all_gather(normed, VIS, axis=0, tiled=True)
    w_out_all = lax.all_gather(w_out, VIS, axis=0, tiled=True)

    weight = (w_kv.astype(F32) * kv_gain[:, None]).astype(BF16)
    text_kv = whole_kv(partial_kv(prompt_text, weight, KVH, parts), shard_rows)

    qkv = jnp.dot(gathered, w_qkv, preferred_element_type=F32).astype(BF16)
    heads = vision_attention(qkv, local_heads)
    returned = lax.all_to_all(heads, VIS, split_axis=0, concat_axis=1, tiled=True)
    projected = jnp.dot(returned, w_out_all, preferred_element_type=F32)
    mixed = floats + projected
    merged = layer_norm(mixed, merge_gain).astype(BF16).reshape(patch_count // 4, MD)
    visual = jnp.dot(
        lax.all_gather(merged, VIS, axis=0, tiled=True), w_merge, preferred_element_type=F32
    ).astype(BF16)
    image_kv = whole_kv(partial_kv(visual, weight, KVH, parts), visual.shape[0])

    flat = (token_dest * shard_rows + token_row).reshape(-1)
    positions = jnp.arange(ctx_count * shard_rows, dtype=jnp.int32)
    taken = jnp.any(positions[:, None] == flat[None, :], axis=1)

    width = KVH * HD
    group = QH // KVH
    mine = QH // vis_count
    resp_rows = queries.shape[0]
    scale = 1.0 / math.sqrt(HD)
    query = lax.dynamic_slice_in_dim(queries, vis_index * mine * HD, mine * HD, 1)
    query = query.reshape(resp_rows, mine, HD).transpose(1, 0, 2).reshape(mine * resp_rows, HD)
    kv_head = (vis_index * mine) // group
    own_keys = lax.dynamic_slice_in_dim(resp_kv, kv_head * HD, HD, 1)
    own_values = lax.dynamic_slice_in_dim(resp_kv, width + kv_head * HD, HD, 1)
    early_keys = jnp.concatenate([text_kv[:, :HD], own_keys], axis=0)
    early_values = jnp.concatenate([text_kv[:, HD:], own_values], axis=0)
    query_positions = jnp.arange(resp_rows, dtype=jnp.int32)
    causal = query_positions[None, :] <= query_positions[:, None]
    visible = jnp.concatenate(
        [jnp.broadcast_to(~taken[None, :], (resp_rows, taken.shape[0])), causal], axis=1
    )
    visible = jnp.broadcast_to(visible[None], (mine,) + visible.shape).reshape(
        mine * resp_rows, -1
    )

    def scores_of(keys):
        return jnp.einsum("qd,kd->qk", query, keys, preferred_element_type=F32) * scale

    scores = jnp.where(visible, scores_of(early_keys), -1e30)
    early_high = jnp.max(scores, axis=1, keepdims=True)
    expo = jnp.where(visible, jnp.exp(scores - early_high), 0.0)
    early_sum = jnp.sum(expo, axis=1, keepdims=True)
    early_mix = jnp.dot(expo.astype(BF16), early_values, preferred_element_type=F32)

    late_scores = scores_of(image_kv[:, :HD])
    high = jnp.maximum(early_high, jnp.max(late_scores, axis=1, keepdims=True))
    late = jnp.exp(late_scores - high)
    fade = jnp.exp(early_high - high)
    summed = early_sum * fade + jnp.sum(late, axis=1, keepdims=True)
    mix = early_mix * fade + jnp.dot(
        late.astype(BF16), image_kv[:, HD:], preferred_element_type=F32
    )
    live = jnp.tile(query_positions < resp_len[0], mine)[:, None]
    result = jnp.where(live, mix / summed, 0.0).astype(BF16)
    result = result.reshape(mine, resp_rows, HD)
    whole = lax.all_gather(result, VIS, axis=0, tiled=True)
    return whole.transpose(1, 0, 2).reshape(resp_rows, QH * HD)


def solution(mesh):
    ctx_count, vis_count = mesh.shape["ctx"], mesh.shape["vis"]
    parts = max(1, vis_count // KVH)
    fine = Mesh(mesh.devices.reshape(ctx_count, vis_count // parts, parts), ("ctx", "vk", "vg"))
    return jax.shard_map(
        per_device,
        mesh=fine,
        in_specs=(
            P(("ctx",) + VIS, None),
            P(),
            P(None, VIS),
            P(VIS, None),
            P(),
            P(None, VIS),
            P(),
            P(),
            P("ctx", VIS),
            P(VIS),
            P(VIS, None),
            P("ctx", None),
            P("ctx", None),
            P("ctx"),
        ),
        out_specs=P("ctx", None),
        check_vma=False,
    )
```

```python
import functools
import math

import jax
import jax.numpy as jnp
from jax import lax
from jax.experimental import pallas as pl
from jax.experimental.pallas import tpu as pltpu
from jax.sharding import Mesh, PartitionSpec as P

VD = 1280
VHEADS = 16
D = 8192
HD = 128
QH = 32
KVH = 4
VHD = 80
MD = 5120


EPS = 1e-06
VIS = ("vk", "vh", "core")
SUB = ("vh", "core")
MESH = pl.DeviceIdType.MESH
VMEM = pl.BlockSpec(memory_space=pltpu.VMEM)
F32 = jnp.float32
BF16 = jnp.bfloat16


def layer_norm(values, gain):
    center = values - jnp.mean(values, axis=-1, keepdims=True)
    spread = jnp.mean(center * center, axis=-1, keepdims=True)
    return center * lax.rsqrt(spread + EPS) * gain


def vision_attention(qkv, local_heads):
    scale = 1.0 / math.sqrt(VHD)
    outs = []
    for h in range(local_heads):
        base = h * 3 * VHD
        query = qkv[:, base : base + VHD]
        keys = qkv[:, base + VHD : base + 2 * VHD]
        values = qkv[:, base + 2 * VHD : base + 3 * VHD]
        scores = jnp.einsum("qd,kd->qk", query, keys, preferred_element_type=F32) * scale
        expo = jnp.exp(scores - jnp.max(scores, axis=1, keepdims=True))
        summed = jnp.sum(expo, axis=1, keepdims=True)
        mixed = jnp.einsum("qk,kd->dq", expo.astype(BF16), values, preferred_element_type=F32)
        outs.append((mixed / summed.reshape(1, -1)).astype(BF16))
    return jnp.concatenate(outs, axis=0)


def flat_index(names, sizes):
    index = 0
    for name, size in zip(names, sizes):
        index = index * size + lax.axis_index(name)
    return index


def coordinates(index, names, sizes):
    place = {}
    for name, size in reversed(list(zip(names, sizes))):
        place[name] = index % size
        index = index // size
    return place


def exchange_kernel(names, sizes, spread, count, *refs):
    xs, outs = refs[:count], refs[count : 2 * count]
    send_sem, recv_sem, local_sem = refs[2 * count :]
    total = math.prod(sizes)
    me = flat_index(names, sizes)
    barrier = pltpu.get_barrier_semaphore()
    for step in range(1, total):
        pl.semaphore_signal(
            barrier,
            inc=1,
            device_id=coordinates((me + step) % total, names, sizes),
            device_id_type=MESH,
        )
    pl.semaphore_wait(barrier, total - 1)
    copies = []
    for step in range(1, total):
        target = (me + step) % total
        for i in range(count):
            copy = pltpu.make_async_remote_copy(
                src_ref=xs[i] if spread else xs[i].at[target],
                dst_ref=outs[i].at[me],
                send_sem=send_sem.at[i, step],
                recv_sem=recv_sem.at[i, step],
                device_id=coordinates(target, names, sizes),
                device_id_type=MESH,
            )
            copy.start()
            copies.append(copy)
    for i in range(count):
        own = pltpu.make_async_copy(
            xs[i] if spread else xs[i].at[me], outs[i].at[me], local_sem.at[i]
        )
        own.start()
        copies.append(own)
    for copy in copies:
        copy.wait()


def exchange(xs, names, spread, collective_id):
    sizes = tuple(lax.axis_size(name) for name in names)
    total, count = math.prod(sizes), len(xs)
    shapes = [((total,) + x.shape) if spread else x.shape for x in xs]
    return pl.pallas_call(
        functools.partial(exchange_kernel, names, sizes, spread, count),
        out_shape=[jax.ShapeDtypeStruct(sh, x.dtype) for sh, x in zip(shapes, xs)],
        in_specs=[VMEM] * count,
        out_specs=[VMEM] * count,
        scratch_shapes=[
            pltpu.SemaphoreType.DMA((count, total)),
            pltpu.SemaphoreType.DMA((count, total)),
            pltpu.SemaphoreType.DMA((count,)),
        ],
        compiler_params=pltpu.CompilerParams(
            collective_id=collective_id, has_side_effects=True
        ),
        cost_estimate=pl.CostEstimate(flops=0, bytes_accessed=30_000_000, transcendentals=0),
    )(*xs)


def line_kernel(sizes, chunks, x_ref, out_ref, send_sem, recv_sem, share_send, share_recv, local_sem):
    chips = sizes[0] * sizes[1]
    core = lax.axis_index("core")
    chip = lax.axis_index("vk") * sizes[1] + lax.axis_index("vh")
    rows = x_ref.shape[0] // chunks

    def at(where, which):
        return {"vk": where // sizes[1], "vh": where % sizes[1], "core": which}

    def neighbour(direction):
        return chip + 1 if direction == 0 else chip - 1

    def has(direction):
        return chip < chips - 1 if direction == 0 else chip > 0

    barrier = pltpu.get_barrier_semaphore()
    pl.semaphore_signal(barrier, inc=1, device_id=at(chip, 1 - core), device_id_type=MESH)
    for direction in range(2):
        @pl.when(has(direction))
        def _():
            pl.semaphore_signal(
                barrier, inc=1, device_id=at(neighbour(direction), core), device_id_type=MESH
            )
    pl.semaphore_wait(barrier, 1 + jnp.where(has(0), 1, 0) + jnp.where(has(1), 1, 0))

    def slot(origin, which, piece):
        return out_ref.at[origin * 2 + which, pl.ds(piece * rows, rows)]

    def source(origin, piece, hop):
        return x_ref.at[pl.ds(piece * rows, rows)] if hop == 0 else slot(origin, core, piece)

    def origin_of(direction, hop):
        return chip - hop if direction == 0 else chip + hop

    def exists(direction, hop):
        return chip >= hop if direction == 0 else chip + hop < chips

    def pass_on(direction, hop, piece):
        origin = origin_of(direction, hop)
        return pltpu.make_async_remote_copy(
            src_ref=source(origin, piece, hop),
            dst_ref=slot(origin, core, piece),
            send_sem=send_sem.at[direction, hop, piece],
            recv_sem=recv_sem.at[direction, hop, piece],
            device_id=at(neighbour(direction), core),
            device_id_type=MESH,
        )

    def arrival(direction, hop, piece):
        origin = origin_of(direction, hop)
        return pltpu.make_async_remote_copy(
            src_ref=slot(origin, core, piece),
            dst_ref=slot(origin, core, piece),
            send_sem=send_sem.at[direction, hop - 1, piece],
            recv_sem=recv_sem.at[direction, hop - 1, piece],
            device_id=at(chip, 1 - core),
            device_id_type=MESH,
        )

    def share(origin, piece, hop):
        return pltpu.make_async_remote_copy(
            src_ref=source(origin, piece, hop),
            dst_ref=slot(origin, core, piece),
            send_sem=share_send.at[origin, piece],
            recv_sem=share_recv.at[origin, piece],
            device_id=at(chip, 1 - core),
            device_id_type=MESH,
        )

    for piece in range(chunks):
        for direction in range(2):
            @pl.when(has(direction))
            def _():
                pass_on(direction, 0, piece).start()
    own = pltpu.make_async_copy(x_ref, out_ref.at[chip * 2 + core], local_sem)
    own.start()
    for piece in range(chunks):
        share(chip, piece, 0).start()
    for hop in range(1, chips):
        for piece in range(chunks):
            for direction in range(2):
                @pl.when(exists(direction, hop))
                def _():
                    arrival(direction, hop, piece).wait_recv()
                    if hop < chips - 1:
                        @pl.when(has(direction))
                        def _():
                            pass_on(direction, hop, piece).start()
                    share(origin_of(direction, hop), piece, hop).start()
    own.wait()
    for piece in range(chunks):
        share(chip, piece, 0).wait_send()
        for direction in range(2):
            for hop in range(chips):
                if hop < chips - 1:
                    @pl.when(jnp.logical_and(exists(direction, hop), has(direction)))
                    def _():
                        pass_on(direction, hop, piece).wait_send()
                if hop > 0:
                    @pl.when(exists(direction, hop))
                    def _():
                        share(origin_of(direction, hop), piece, hop).wait_send()
        for origin in range(chips):
            pltpu.make_async_remote_copy(
                src_ref=slot(origin, 1 - core, piece),
                dst_ref=slot(origin, 1 - core, piece),
                send_sem=share_send.at[origin, piece],
                recv_sem=share_recv.at[origin, piece],
                device_id=at(chip, 1 - core),
                device_id_type=MESH,
            ).wait_recv()


def line_gather(x, chunks, collective_id):
    sizes = tuple(lax.axis_size(name) for name in VIS)
    chips = sizes[0] * sizes[1]
    return pl.pallas_call(
        functools.partial(line_kernel, sizes, chunks),
        out_shape=jax.ShapeDtypeStruct((2 * chips,) + x.shape, x.dtype),
        in_specs=[VMEM],
        out_specs=VMEM,
        scratch_shapes=[
            pltpu.SemaphoreType.DMA((2, chips, chunks)),
            pltpu.SemaphoreType.DMA((2, chips, chunks)),
            pltpu.SemaphoreType.DMA((chips, chunks)),
            pltpu.SemaphoreType.DMA((chips, chunks)),
            pltpu.SemaphoreType.DMA,
        ],
        compiler_params=pltpu.CompilerParams(
            collective_id=collective_id, has_side_effects=True
        ),
        cost_estimate=pl.CostEstimate(flops=0, bytes_accessed=70_000_000, transcendentals=0),
    )(x)


def text_kernel(rows_ref, weight_ref, out_ref):
    rows = rows_ref[...]
    each = rows.shape[0]
    out_ref[0, :each, :] = jnp.dot(rows, weight_ref[0], preferred_element_type=F32)
    floats = rows.astype(F32)
    squares = floats * floats
    coarse = squares.astype(BF16)
    rest = (squares - coarse.astype(F32)).astype(BF16)
    ones = jnp.ones((8, rows.shape[1]), BF16)
    dims = (((1,), (1,)), ((), ()))
    sums = lax.dot_general(ones, coarse, dims, preferred_element_type=F32)
    sums += lax.dot_general(ones, rest, dims, preferred_element_type=F32)
    out_ref[0, each:, :] = sums[:, : 2 * HD]
    for part in range(1, each // (2 * HD)):
        out_ref[0, each + part : each + part + 1, :] = sums[:1, part * 2 * HD : (part + 1) * 2 * HD]


def text_partial(text, weight, parts):
    count, depth = text.shape
    each = count // parts
    return pl.pallas_call(
        text_kernel,
        grid=(parts, KVH),
        out_shape=jax.ShapeDtypeStruct((KVH * parts, each + 8, 2 * HD), F32),
        in_specs=[
            pl.BlockSpec((each, depth), lambda p, h: (p, 0)),
            pl.BlockSpec((1, depth, 2 * HD), lambda p, h: (h, 0, 0)),
        ],
        out_specs=pl.BlockSpec((1, each + 8, 2 * HD), lambda p, h: (h * parts + p, 0, 0)),
        cost_estimate=pl.CostEstimate(
            flops=2 * count * depth * KVH * 2 * HD,
            bytes_accessed=10_000_000,
            transcendentals=0,
        ),
    )(text, weight)


def whole_text(partial):
    total = lax.psum_scatter(partial, VIS, scatter_dimension=0, tiled=True)[0]
    each = total.shape[0] - 8
    squares = total[each : each + each // (2 * HD)].reshape(each)
    inverse = lax.rsqrt(squares / D + EPS)
    share = (total[:each] * inverse[:, None]).astype(BF16)
    return lax.all_gather(share, ("ctx",) + SUB, axis=0, tiled=True)


def whole_image(visual, weight, parts):
    each = visual.shape[0] // parts
    raw = jnp.einsum("rd,hde->hre", visual, weight, preferred_element_type=F32)
    pieces = raw.astype(BF16).reshape(KVH * parts, each, 2 * HD)
    floats = visual.astype(F32)
    squares = jnp.sum(floats * floats, axis=1).reshape(1, parts, 1, each)
    squares = jnp.broadcast_to(squares, (KVH, parts, 8, each)).reshape(KVH * parts, 8, each)
    pieces, squares = exchange((pieces, squares), VIS, False, 3)
    total = jnp.sum(pieces.astype(F32), axis=0)
    inverse = lax.rsqrt(jnp.sum(squares[:, 0, :], axis=0) / D + EPS)
    share = (total * inverse[:, None]).astype(BF16)
    (whole,) = exchange((share,), ("ctx",) + SUB, True, 4)
    return whole.reshape(-1, 2 * HD)


def per_device(
    patches,
    vis_gain,
    w_qkv,
    w_out,
    merge_gain,
    w_merge,
    token_dest,
    token_row,
    prompt_text,
    kv_gain,
    w_kv,
    queries,
    resp_kv,
    resp_len,
):
    parts = lax.axis_size("vh") * lax.axis_size("core")
    vis_count = lax.axis_size("vk") * parts
    ctx_count = lax.axis_size("ctx")
    vis_index = flat_index(VIS, tuple(lax.axis_size(name) for name in VIS))
    patch_count = patches.shape[0]
    shard_rows = prompt_text.shape[0]
    local_heads = VHEADS // vis_count

    floats = patches.astype(F32)
    normed = layer_norm(floats, vis_gain).astype(BF16)
    gathered = line_gather(normed, 2, 0).reshape(-1, VD)
    w_out_all = lax.all_gather(w_out, VIS, axis=0, tiled=True)

    weight = (w_kv.astype(F32) * kv_gain[:, None]).astype(BF16)
    weight = weight.reshape(-1, 2, KVH, HD).transpose(2, 0, 1, 3).reshape(KVH, -1, 2 * HD)
    text_kv = whole_text(text_partial(prompt_text, weight, parts))

    qkv = jnp.dot(gathered, w_qkv, preferred_element_type=F32).astype(BF16)
    heads = vision_attention(qkv, local_heads)
    heads = heads.reshape(-1, vis_count, patch_count).transpose(1, 0, 2)
    (returned,) = exchange((heads,), VIS, False, 1)
    projected = jnp.einsum(
        "dp,de->pe", returned.reshape(VD, patch_count), w_out_all, preferred_element_type=F32
    )
    mixed = floats + projected
    merged = layer_norm(mixed, merge_gain).astype(BF16).reshape(patch_count // 4, MD)
    visual = jnp.dot(
        line_gather(merged, 2, 2).reshape(-1, MD), w_merge, preferred_element_type=F32
    ).astype(BF16)
    image_kv = whole_image(visual, weight, parts)

    flat = (token_dest * shard_rows + token_row).reshape(-1)
    positions = jnp.arange(ctx_count * shard_rows, dtype=jnp.int32)
    taken = jnp.any(positions[:, None] == flat[None, :], axis=1)

    width = KVH * HD
    group = QH // KVH
    mine = QH // vis_count
    resp_rows = queries.shape[0]
    scale = 1.0 / math.sqrt(HD)
    query = lax.dynamic_slice_in_dim(queries, vis_index * mine * HD, mine * HD, 1)
    query = query.reshape(resp_rows, mine, HD).transpose(1, 0, 2).reshape(mine * resp_rows, HD)
    kv_head = (vis_index * mine) // group
    own_keys = lax.dynamic_slice_in_dim(resp_kv, kv_head * HD, HD, 1)
    own_values = lax.dynamic_slice_in_dim(resp_kv, width + kv_head * HD, HD, 1)
    early_keys = jnp.concatenate([text_kv[:, :HD], own_keys], axis=0)
    early_values = jnp.concatenate([text_kv[:, HD:], own_values], axis=0)
    query_positions = jnp.arange(resp_rows, dtype=jnp.int32)
    causal = query_positions[None, :] <= query_positions[:, None]
    visible = jnp.concatenate(
        [jnp.broadcast_to(~taken[None, :], (resp_rows, taken.shape[0])), causal], axis=1
    )
    visible = jnp.broadcast_to(visible[None], (mine,) + visible.shape).reshape(
        mine * resp_rows, -1
    )

    def scores_of(keys):
        return jnp.einsum("qd,kd->qk", query, keys, preferred_element_type=F32) * scale

    scores = jnp.where(visible, scores_of(early_keys), -1e30)
    early_high = jnp.max(scores, axis=1, keepdims=True)
    expo = jnp.where(visible, jnp.exp(scores - early_high), 0.0)
    early_sum = jnp.sum(expo, axis=1, keepdims=True)
    early_mix = jnp.dot(expo.astype(BF16), early_values, preferred_element_type=F32)

    late_scores = scores_of(image_kv[:, :HD])
    high = jnp.maximum(early_high, jnp.max(late_scores, axis=1, keepdims=True))
    late = jnp.exp(late_scores - high)
    fade = jnp.exp(early_high - high)
    summed = early_sum * fade + jnp.sum(late, axis=1, keepdims=True)
    mix = early_mix * fade + jnp.dot(
        late.astype(BF16), image_kv[:, HD:], preferred_element_type=F32
    )
    live = jnp.tile(query_positions < resp_len[0], mine)[:, None]
    result = jnp.where(live, mix / summed, 0.0).astype(BF16)
    result = result.reshape(mine, resp_rows, HD).transpose(1, 0, 2)
    whole = line_gather(result.reshape(resp_rows, mine * HD), 2, 5)
    return whole.transpose(1, 0, 2).reshape(resp_rows, QH * HD)


def solution(mesh):
    ctx_count, vis_count = mesh.shape["ctx"], mesh.shape["vis"]
    parts = vis_count // KVH
    shape = (ctx_count, vis_count // parts, parts // 2, 2)
    fine = Mesh(mesh.devices.reshape(shape), ("ctx",) + VIS)
    return jax.shard_map(
        per_device,
        mesh=fine,
        in_specs=(
            P(("ctx",) + VIS, None),
            P(),
            P(None, VIS),
            P(VIS, None),
            P(),
            P(None, VIS),
            P(),
            P(),
            P("ctx", VIS),
            P(VIS),
            P(VIS, None),
            P("ctx", None),
            P("ctx", None),
            P("ctx"),
        ),
        out_specs=P("ctx", None),
        check_vma=False,
    )
```

```python
import functools
import math

import jax
import jax.numpy as jnp
from jax import lax
from jax.experimental import pallas as pl
from jax.experimental.pallas import tpu as pltpu
from jax.sharding import Mesh, PartitionSpec as P

VD = 1280
VHEADS = 16
D = 8192
HD = 128
QH = 32
KVH = 4
VHD = 80
MD = 5120


EPS = 1e-06
VIS = ("vk", "vh", "core")
SUB = ("vh", "core")
MESH = pl.DeviceIdType.MESH
VMEM = pl.BlockSpec(memory_space=pltpu.VMEM)
F32 = jnp.float32
BF16 = jnp.bfloat16


def layer_norm(values, gain):
    center = values - jnp.mean(values, axis=-1, keepdims=True)
    spread = jnp.mean(center * center, axis=-1, keepdims=True)
    return center * lax.rsqrt(spread + EPS) * gain


def vision_attention(qkv, local_heads):
    scale = 1.0 / math.sqrt(VHD)
    outs = []
    for h in range(local_heads):
        base = h * 3 * VHD
        query = qkv[:, base : base + VHD]
        keys = qkv[:, base + VHD : base + 2 * VHD]
        values = qkv[:, base + 2 * VHD : base + 3 * VHD]
        scores = jnp.einsum("qd,kd->qk", query, keys, preferred_element_type=F32) * scale
        expo = jnp.exp(scores - jnp.max(scores, axis=1, keepdims=True))
        summed = jnp.sum(expo, axis=1, keepdims=True)
        mixed = jnp.einsum("qk,kd->dq", expo.astype(BF16), values, preferred_element_type=F32)
        outs.append((mixed / summed.reshape(1, -1)).astype(BF16))
    return jnp.concatenate(outs, axis=0)


def flat_index(names, sizes):
    index = 0
    for name, size in zip(names, sizes):
        index = index * size + lax.axis_index(name)
    return index


def coordinates(index, names, sizes):
    place = {}
    for name, size in reversed(list(zip(names, sizes))):
        place[name] = index % size
        index = index // size
    return place


def exchange_kernel(names, sizes, spread, count, *refs):
    xs, outs = refs[:count], refs[count : 2 * count]
    send_sem, recv_sem, local_sem = refs[2 * count :]
    total = math.prod(sizes)
    me = flat_index(names, sizes)
    barrier = pltpu.get_barrier_semaphore()
    for step in range(1, total):
        pl.semaphore_signal(
            barrier,
            inc=1,
            device_id=coordinates((me + step) % total, names, sizes),
            device_id_type=MESH,
        )
    pl.semaphore_wait(barrier, total - 1)
    copies = []
    for step in range(1, total):
        target = (me + step) % total
        for i in range(count):
            copy = pltpu.make_async_remote_copy(
                src_ref=xs[i] if spread else xs[i].at[target],
                dst_ref=outs[i].at[me],
                send_sem=send_sem.at[i, step],
                recv_sem=recv_sem.at[i, step],
                device_id=coordinates(target, names, sizes),
                device_id_type=MESH,
            )
            copy.start()
            copies.append(copy)
    for i in range(count):
        own = pltpu.make_async_copy(
            xs[i] if spread else xs[i].at[me], outs[i].at[me], local_sem.at[i]
        )
        own.start()
        copies.append(own)
    for copy in copies:
        copy.wait()


def exchange(xs, names, spread, collective_id):
    sizes = tuple(lax.axis_size(name) for name in names)
    total, count = math.prod(sizes), len(xs)
    shapes = [((total,) + x.shape) if spread else x.shape for x in xs]
    return pl.pallas_call(
        functools.partial(exchange_kernel, names, sizes, spread, count),
        out_shape=[jax.ShapeDtypeStruct(sh, x.dtype) for sh, x in zip(shapes, xs)],
        in_specs=[VMEM] * count,
        out_specs=[VMEM] * count,
        scratch_shapes=[
            pltpu.SemaphoreType.DMA((count, total)),
            pltpu.SemaphoreType.DMA((count, total)),
            pltpu.SemaphoreType.DMA((count,)),
        ],
        compiler_params=pltpu.CompilerParams(
            collective_id=collective_id, has_side_effects=True
        ),
        cost_estimate=pl.CostEstimate(flops=0, bytes_accessed=30_000_000, transcendentals=0),
    )(*xs)


def line_kernel(sizes, chunks, x_ref, out_ref, send_sem, recv_sem, share_send, share_recv, local_sem):
    chips = sizes[0] * sizes[1]
    core = lax.axis_index("core")
    chip = lax.axis_index("vk") * sizes[1] + lax.axis_index("vh")
    rows = x_ref.shape[0] // chunks

    def at(where, which):
        return {"vk": where // sizes[1], "vh": where % sizes[1], "core": which}

    def neighbour(direction):
        return chip + 1 if direction == 0 else chip - 1

    def has(direction):
        return chip < chips - 1 if direction == 0 else chip > 0

    barrier = pltpu.get_barrier_semaphore()
    pl.semaphore_signal(barrier, inc=1, device_id=at(chip, 1 - core), device_id_type=MESH)
    for direction in range(2):
        @pl.when(has(direction))
        def _():
            pl.semaphore_signal(
                barrier, inc=1, device_id=at(neighbour(direction), core), device_id_type=MESH
            )
    pl.semaphore_wait(barrier, 1 + jnp.where(has(0), 1, 0) + jnp.where(has(1), 1, 0))

    def slot(origin, which, piece):
        return out_ref.at[origin * 2 + which, pl.ds(piece * rows, rows)]

    def source(origin, piece, hop):
        return x_ref.at[pl.ds(piece * rows, rows)] if hop == 0 else slot(origin, core, piece)

    def origin_of(direction, hop):
        return chip - hop if direction == 0 else chip + hop

    def exists(direction, hop):
        return chip >= hop if direction == 0 else chip + hop < chips

    def pass_on(direction, hop, piece):
        origin = origin_of(direction, hop)
        return pltpu.make_async_remote_copy(
            src_ref=source(origin, piece, hop),
            dst_ref=slot(origin, core, piece),
            send_sem=send_sem.at[direction, hop, piece],
            recv_sem=recv_sem.at[direction, hop, piece],
            device_id=at(neighbour(direction), core),
            device_id_type=MESH,
        )

    def arrival(direction, hop, piece):
        origin = origin_of(direction, hop)
        return pltpu.make_async_remote_copy(
            src_ref=slot(origin, core, piece),
            dst_ref=slot(origin, core, piece),
            send_sem=send_sem.at[direction, hop - 1, piece],
            recv_sem=recv_sem.at[direction, hop - 1, piece],
            device_id=at(chip, 1 - core),
            device_id_type=MESH,
        )

    def share(origin, piece, hop):
        return pltpu.make_async_remote_copy(
            src_ref=source(origin, piece, hop),
            dst_ref=slot(origin, core, piece),
            send_sem=share_send.at[origin, piece],
            recv_sem=share_recv.at[origin, piece],
            device_id=at(chip, 1 - core),
            device_id_type=MESH,
        )

    for piece in range(chunks):
        for direction in range(2):
            @pl.when(has(direction))
            def _():
                pass_on(direction, 0, piece).start()
    own = pltpu.make_async_copy(x_ref, out_ref.at[chip * 2 + core], local_sem)
    own.start()
    for piece in range(chunks):
        share(chip, piece, 0).start()
    for hop in range(1, chips):
        for piece in range(chunks):
            for direction in range(2):
                @pl.when(exists(direction, hop))
                def _():
                    arrival(direction, hop, piece).wait_recv()
                    if hop < chips - 1:
                        @pl.when(has(direction))
                        def _():
                            pass_on(direction, hop, piece).start()
                    share(origin_of(direction, hop), piece, hop).start()
    own.wait()
    for piece in range(chunks):
        share(chip, piece, 0).wait_send()
        for direction in range(2):
            for hop in range(chips):
                if hop < chips - 1:
                    @pl.when(jnp.logical_and(exists(direction, hop), has(direction)))
                    def _():
                        pass_on(direction, hop, piece).wait_send()
                if hop > 0:
                    @pl.when(exists(direction, hop))
                    def _():
                        share(origin_of(direction, hop), piece, hop).wait_send()
        for origin in range(chips):
            pltpu.make_async_remote_copy(
                src_ref=slot(origin, 1 - core, piece),
                dst_ref=slot(origin, 1 - core, piece),
                send_sem=share_send.at[origin, piece],
                recv_sem=share_recv.at[origin, piece],
                device_id=at(chip, 1 - core),
                device_id_type=MESH,
            ).wait_recv()


def line_gather(x, chunks, collective_id):
    sizes = tuple(lax.axis_size(name) for name in VIS)
    chips = sizes[0] * sizes[1]
    return pl.pallas_call(
        functools.partial(line_kernel, sizes, chunks),
        out_shape=jax.ShapeDtypeStruct((2 * chips,) + x.shape, x.dtype),
        in_specs=[VMEM],
        out_specs=VMEM,
        scratch_shapes=[
            pltpu.SemaphoreType.DMA((2, chips, chunks)),
            pltpu.SemaphoreType.DMA((2, chips, chunks)),
            pltpu.SemaphoreType.DMA((chips, chunks)),
            pltpu.SemaphoreType.DMA((chips, chunks)),
            pltpu.SemaphoreType.DMA,
        ],
        compiler_params=pltpu.CompilerParams(
            collective_id=collective_id, has_side_effects=True
        ),
        cost_estimate=pl.CostEstimate(flops=0, bytes_accessed=70_000_000, transcendentals=0),
    )(x)


def project_kernel(joined, rows_ref, key_ref, value_ref, out_ref, *rest):
    sums_ref = rest[-1]
    each = rows_ref.shape[0]
    rows = rows_ref[...]

    @pl.when(pl.program_id(1) == 0)
    def _():
        floats = rows.astype(F32)
        squares = floats * floats
        coarse = squares.astype(BF16)
        fine = (squares - coarse.astype(F32)).astype(BF16)
        ones = jnp.ones((8, rows.shape[1]), BF16)
        dims = (((1,), (1,)), ((), ()))
        sums_ref[...] = lax.dot_general(
            ones, coarse, dims, preferred_element_type=F32
        ) + lax.dot_general(ones, fine, dims, preferred_element_type=F32)

    both = jnp.concatenate([key_ref[...], value_ref[...]], axis=1)
    raw = jnp.dot(rows, both, preferred_element_type=F32)
    if joined:
        out_ref[0, :each, :] = raw
        out_ref[0, each:, :] = sums_ref[:, : 2 * HD]
        for part in range(1, each // (2 * HD)):
            out_ref[0, each + part : each + part + 1, :] = sums_ref[
                :1, part * 2 * HD : (part + 1) * 2 * HD
            ]
    else:
        out_ref[0] = raw.astype(BF16)
        rest[0][0] = sums_ref[...]


def project(rows, weight, parts, joined):
    count, depth = rows.shape
    each = count // parts
    pieces = KVH * parts
    place = lambda p, h: (h * parts + p, 0, 0)
    if joined:
        shapes = [jax.ShapeDtypeStruct((pieces, each + 8, 2 * HD), F32)]
    else:
        shapes = [
            jax.ShapeDtypeStruct((pieces, each, 2 * HD), BF16),
            jax.ShapeDtypeStruct((pieces, 8, each), F32),
        ]
    return pl.pallas_call(
        functools.partial(project_kernel, joined),
        grid=(parts, KVH),
        out_shape=shapes,
        in_specs=[
            pl.BlockSpec((each, depth), lambda p, h: (p, 0)),
            pl.BlockSpec((depth, HD), lambda p, h: (0, h)),
            pl.BlockSpec((depth, HD), lambda p, h: (0, KVH + h)),
        ],
        out_specs=[pl.BlockSpec((1,) + shape.shape[1:], place) for shape in shapes],
        scratch_shapes=[pltpu.VMEM((8, each), F32)],
        cost_estimate=pl.CostEstimate(
            flops=2 * count * depth * KVH * 2 * HD,
            bytes_accessed=count * depth * 10,
            transcendentals=0,
        ),
    )(rows, weight, weight)


def whole_text(total):
    total = total[0]
    each = total.shape[0] - 8
    squares = total[each : each + each // (2 * HD)].reshape(each)
    inverse = lax.rsqrt(squares / D + EPS)
    share = (total[:each] * inverse[:, None]).astype(BF16)
    return lax.all_gather(share, ("ctx",) + SUB, axis=0, tiled=True)


def whole_image(visual, weight, parts):
    pieces, squares = project(visual, weight, parts, False)
    pieces, squares = exchange((pieces, squares), VIS, False, 3)
    total = jnp.sum(pieces.astype(F32), axis=0)
    inverse = lax.rsqrt(jnp.sum(squares[:, 0, :], axis=0) / D + EPS)
    share = (total * inverse[:, None]).astype(BF16)
    (whole,) = exchange((share,), ("ctx",) + SUB, True, 4)
    return whole.reshape(-1, 2 * HD)


def per_device(
    patches,
    vis_gain,
    w_qkv,
    w_out,
    merge_gain,
    w_merge,
    token_dest,
    token_row,
    prompt_text,
    kv_gain,
    w_kv,
    queries,
    resp_kv,
    resp_len,
):
    parts = lax.axis_size("vh") * lax.axis_size("core")
    vis_count = lax.axis_size("vk") * parts
    ctx_count = lax.axis_size("ctx")
    vis_index = flat_index(VIS, tuple(lax.axis_size(name) for name in VIS))
    patch_count = patches.shape[0]
    shard_rows = prompt_text.shape[0]
    local_heads = VHEADS // vis_count

    floats = patches.astype(F32)
    normed = layer_norm(floats, vis_gain).astype(BF16)
    gathered = line_gather(normed, 2, 0).reshape(-1, VD)
    w_out_all = lax.all_gather(w_out, VIS, axis=0, tiled=True)

    weight = (w_kv.astype(F32) * kv_gain[:, None]).astype(BF16)
    weight, gathered, w_out_all = lax.optimization_barrier((weight, gathered, w_out_all))
    text_total = lax.psum_scatter(
        project(prompt_text, weight, parts, True)[0], VIS, scatter_dimension=0, tiled=True
    )

    qkv = jnp.dot(gathered, w_qkv, preferred_element_type=F32).astype(BF16)
    heads = vision_attention(qkv, local_heads)
    heads = heads.reshape(-1, vis_count, patch_count).transpose(1, 0, 2)
    (returned,) = exchange((heads,), VIS, False, 1)
    projected = jnp.einsum(
        "dp,de->pe", returned.reshape(VD, patch_count), w_out_all, preferred_element_type=F32
    )
    mixed = floats + projected
    merged = layer_norm(mixed, merge_gain).astype(BF16).reshape(patch_count // 4, MD)
    merged = line_gather(merged, 2, 2).reshape(-1, MD)
    merged, text_total = lax.optimization_barrier((merged, text_total))
    text_kv = whole_text(text_total)
    visual = jnp.dot(merged, w_merge, preferred_element_type=F32).astype(BF16)
    image_kv = whole_image(visual, weight, parts)

    flat = (token_dest * shard_rows + token_row).reshape(-1)
    positions = jnp.arange(ctx_count * shard_rows, dtype=jnp.int32)
    taken = jnp.any(positions[:, None] == flat[None, :], axis=1)

    width = KVH * HD
    group = QH // KVH
    mine = QH // vis_count
    resp_rows = queries.shape[0]
    scale = 1.0 / math.sqrt(HD)
    query = lax.dynamic_slice_in_dim(queries, vis_index * mine * HD, mine * HD, 1)
    query = query.reshape(resp_rows, mine, HD).transpose(1, 0, 2).reshape(mine * resp_rows, HD)
    kv_head = (vis_index * mine) // group
    own_keys = lax.dynamic_slice_in_dim(resp_kv, kv_head * HD, HD, 1)
    own_values = lax.dynamic_slice_in_dim(resp_kv, width + kv_head * HD, HD, 1)
    early_keys = jnp.concatenate([text_kv[:, :HD], own_keys], axis=0)
    early_values = jnp.concatenate([text_kv[:, HD:], own_values], axis=0)
    query_positions = jnp.arange(resp_rows, dtype=jnp.int32)
    causal = query_positions[None, :] <= query_positions[:, None]
    visible = jnp.concatenate(
        [jnp.broadcast_to(~taken[None, :], (resp_rows, taken.shape[0])), causal], axis=1
    )
    visible = jnp.broadcast_to(visible[None], (mine,) + visible.shape).reshape(
        mine * resp_rows, -1
    )

    def scores_of(keys):
        return jnp.einsum("qd,kd->qk", query, keys, preferred_element_type=F32) * scale

    scores = jnp.where(visible, scores_of(early_keys), -1e30)
    early_high = jnp.max(scores, axis=1, keepdims=True)
    expo = jnp.where(visible, jnp.exp(scores - early_high), 0.0)
    early_sum = jnp.sum(expo, axis=1, keepdims=True)
    early_mix = jnp.dot(expo.astype(BF16), early_values, preferred_element_type=F32)

    late_scores = scores_of(image_kv[:, :HD])
    high = jnp.maximum(early_high, jnp.max(late_scores, axis=1, keepdims=True))
    late = jnp.exp(late_scores - high)
    fade = jnp.exp(early_high - high)
    summed = early_sum * fade + jnp.sum(late, axis=1, keepdims=True)
    mix = early_mix * fade + jnp.dot(
        late.astype(BF16), image_kv[:, HD:], preferred_element_type=F32
    )
    live = jnp.tile(query_positions < resp_len[0], mine)[:, None]
    result = jnp.where(live, mix / summed, 0.0).astype(BF16)
    result = result.reshape(mine, resp_rows, HD).transpose(1, 0, 2)
    whole = line_gather(result.reshape(resp_rows, mine * HD), 2, 5)
    return whole.transpose(1, 0, 2).reshape(resp_rows, QH * HD)


def solution(mesh):
    ctx_count, vis_count = mesh.shape["ctx"], mesh.shape["vis"]
    parts = vis_count // KVH
    shape = (ctx_count, vis_count // parts, parts // 2, 2)
    fine = Mesh(mesh.devices.reshape(shape), ("ctx",) + VIS)
    return jax.shard_map(
        per_device,
        mesh=fine,
        in_specs=(
            P(("ctx",) + VIS, None),
            P(),
            P(None, VIS),
            P(VIS, None),
            P(),
            P(None, VIS),
            P(),
            P(),
            P("ctx", VIS),
            P(VIS),
            P(VIS, None),
            P("ctx", None),
            P("ctx", None),
            P("ctx"),
        ),
        out_specs=P("ctx", None),
        check_vma=False,
    )
```

```python
import functools
import math

import jax
import jax.numpy as jnp
from jax import lax
from jax.experimental import pallas as pl
from jax.experimental.pallas import tpu as pltpu
from jax.sharding import Mesh, PartitionSpec as P

VD = 1280
VHEADS = 16
D = 8192
HD = 128
QH = 32
KVH = 4
VHD = 80
MD = 5120


EPS = 1e-06
VIS = ("vk", "vh", "core")
SUB = ("vh", "core")
MESH = pl.DeviceIdType.MESH
VMEM = pl.BlockSpec(memory_space=pltpu.VMEM)
F32 = jnp.float32
BF16 = jnp.bfloat16


def layer_norm(values, gain):
    center = values - jnp.mean(values, axis=-1, keepdims=True)
    spread = jnp.mean(center * center, axis=-1, keepdims=True)
    return center * lax.rsqrt(spread + EPS) * gain


def vision_attention(qkv, local_heads):
    scale = 1.0 / math.sqrt(VHD)
    outs = []
    for h in range(local_heads):
        base = h * 3 * VHD
        query = qkv[:, base : base + VHD]
        keys = qkv[:, base + VHD : base + 2 * VHD]
        values = qkv[:, base + 2 * VHD : base + 3 * VHD]
        scores = jnp.einsum("qd,kd->qk", query, keys, preferred_element_type=F32) * scale
        expo = jnp.exp(scores - jnp.max(scores, axis=1, keepdims=True))
        summed = jnp.sum(expo, axis=1, keepdims=True)
        mixed = jnp.einsum("qk,kd->dq", expo.astype(BF16), values, preferred_element_type=F32)
        outs.append((mixed / summed.reshape(1, -1)).astype(BF16))
    return jnp.concatenate(outs, axis=0)


def flat_index(names, sizes):
    index = 0
    for name, size in zip(names, sizes):
        index = index * size + lax.axis_index(name)
    return index


def coordinates(index, names, sizes):
    place = {}
    for name, size in reversed(list(zip(names, sizes))):
        place[name] = index % size
        index = index // size
    return place


def exchange_kernel(names, sizes, spread, count, *refs):
    xs, outs = refs[:count], refs[count : 2 * count]
    send_sem, recv_sem, local_sem = refs[2 * count :]
    total = math.prod(sizes)
    me = flat_index(names, sizes)
    barrier = pltpu.get_barrier_semaphore()
    for step in range(1, total):
        pl.semaphore_signal(
            barrier,
            inc=1,
            device_id=coordinates((me + step) % total, names, sizes),
            device_id_type=MESH,
        )
    pl.semaphore_wait(barrier, total - 1)
    copies = []
    for step in range(1, total):
        target = (me + step) % total
        for i in range(count):
            copy = pltpu.make_async_remote_copy(
                src_ref=xs[i] if spread else xs[i].at[target],
                dst_ref=outs[i].at[me],
                send_sem=send_sem.at[i, step],
                recv_sem=recv_sem.at[i, step],
                device_id=coordinates(target, names, sizes),
                device_id_type=MESH,
            )
            copy.start()
            copies.append(copy)
    for i in range(count):
        own = pltpu.make_async_copy(
            xs[i] if spread else xs[i].at[me], outs[i].at[me], local_sem.at[i]
        )
        own.start()
        copies.append(own)
    for copy in copies:
        copy.wait()


def exchange(xs, names, spread, collective_id):
    sizes = tuple(lax.axis_size(name) for name in names)
    total, count = math.prod(sizes), len(xs)
    shapes = [((total,) + x.shape) if spread else x.shape for x in xs]
    return pl.pallas_call(
        functools.partial(exchange_kernel, names, sizes, spread, count),
        out_shape=[jax.ShapeDtypeStruct(sh, x.dtype) for sh, x in zip(shapes, xs)],
        in_specs=[VMEM] * count,
        out_specs=[VMEM] * count,
        scratch_shapes=[
            pltpu.SemaphoreType.DMA((count, total)),
            pltpu.SemaphoreType.DMA((count, total)),
            pltpu.SemaphoreType.DMA((count,)),
        ],
        compiler_params=pltpu.CompilerParams(
            collective_id=collective_id, has_side_effects=True
        ),
        cost_estimate=pl.CostEstimate(flops=0, bytes_accessed=30_000_000, transcendentals=0),
    )(*xs)


def line_kernel(sizes, chunks, x_ref, out_ref, send_sem, recv_sem, share_send, share_recv, local_sem):
    chips = sizes[0] * sizes[1]
    core = lax.axis_index("core")
    chip = lax.axis_index("vk") * sizes[1] + lax.axis_index("vh")
    rows = x_ref.shape[0] // chunks

    def at(where, which):
        return {"vk": where // sizes[1], "vh": where % sizes[1], "core": which}

    def neighbour(direction):
        return chip + 1 if direction == 0 else chip - 1

    def has(direction):
        return chip < chips - 1 if direction == 0 else chip > 0

    barrier = pltpu.get_barrier_semaphore()
    pl.semaphore_signal(barrier, inc=1, device_id=at(chip, 1 - core), device_id_type=MESH)
    for direction in range(2):
        @pl.when(has(direction))
        def _():
            pl.semaphore_signal(
                barrier, inc=1, device_id=at(neighbour(direction), core), device_id_type=MESH
            )
    pl.semaphore_wait(barrier, 1 + jnp.where(has(0), 1, 0) + jnp.where(has(1), 1, 0))

    def slot(origin, which, piece):
        return out_ref.at[origin * 2 + which, pl.ds(piece * rows, rows)]

    def source(origin, piece, hop):
        return x_ref.at[pl.ds(piece * rows, rows)] if hop == 0 else slot(origin, core, piece)

    def origin_of(direction, hop):
        return chip - hop if direction == 0 else chip + hop

    def exists(direction, hop):
        return chip >= hop if direction == 0 else chip + hop < chips

    def pass_on(direction, hop, piece):
        origin = origin_of(direction, hop)
        return pltpu.make_async_remote_copy(
            src_ref=source(origin, piece, hop),
            dst_ref=slot(origin, core, piece),
            send_sem=send_sem.at[direction, hop, piece],
            recv_sem=recv_sem.at[direction, hop, piece],
            device_id=at(neighbour(direction), core),
            device_id_type=MESH,
        )

    def arrival(direction, hop, piece):
        origin = origin_of(direction, hop)
        return pltpu.make_async_remote_copy(
            src_ref=slot(origin, core, piece),
            dst_ref=slot(origin, core, piece),
            send_sem=send_sem.at[direction, hop - 1, piece],
            recv_sem=recv_sem.at[direction, hop - 1, piece],
            device_id=at(chip, 1 - core),
            device_id_type=MESH,
        )

    def share(origin, piece, hop):
        return pltpu.make_async_remote_copy(
            src_ref=source(origin, piece, hop),
            dst_ref=slot(origin, core, piece),
            send_sem=share_send.at[origin, piece],
            recv_sem=share_recv.at[origin, piece],
            device_id=at(chip, 1 - core),
            device_id_type=MESH,
        )

    for piece in range(chunks):
        for direction in range(2):
            @pl.when(has(direction))
            def _():
                pass_on(direction, 0, piece).start()
    own = pltpu.make_async_copy(x_ref, out_ref.at[chip * 2 + core], local_sem)
    own.start()
    for piece in range(chunks):
        share(chip, piece, 0).start()
    for hop in range(1, chips):
        for piece in range(chunks):
            for direction in range(2):
                @pl.when(exists(direction, hop))
                def _():
                    arrival(direction, hop, piece).wait_recv()
                    if hop < chips - 1:
                        @pl.when(has(direction))
                        def _():
                            pass_on(direction, hop, piece).start()
                    share(origin_of(direction, hop), piece, hop).start()
    own.wait()
    for piece in range(chunks):
        share(chip, piece, 0).wait_send()
        for direction in range(2):
            for hop in range(chips):
                if hop < chips - 1:
                    @pl.when(jnp.logical_and(exists(direction, hop), has(direction)))
                    def _():
                        pass_on(direction, hop, piece).wait_send()
                if hop > 0:
                    @pl.when(exists(direction, hop))
                    def _():
                        share(origin_of(direction, hop), piece, hop).wait_send()
        for origin in range(chips):
            pltpu.make_async_remote_copy(
                src_ref=slot(origin, 1 - core, piece),
                dst_ref=slot(origin, 1 - core, piece),
                send_sem=share_send.at[origin, piece],
                recv_sem=share_recv.at[origin, piece],
                device_id=at(chip, 1 - core),
                device_id_type=MESH,
            ).wait_recv()


def line_gather(x, chunks, collective_id):
    sizes = tuple(lax.axis_size(name) for name in VIS)
    chips = sizes[0] * sizes[1]
    return pl.pallas_call(
        functools.partial(line_kernel, sizes, chunks),
        out_shape=jax.ShapeDtypeStruct((2 * chips,) + x.shape, x.dtype),
        in_specs=[VMEM],
        out_specs=VMEM,
        scratch_shapes=[
            pltpu.SemaphoreType.DMA((2, chips, chunks)),
            pltpu.SemaphoreType.DMA((2, chips, chunks)),
            pltpu.SemaphoreType.DMA((chips, chunks)),
            pltpu.SemaphoreType.DMA((chips, chunks)),
            pltpu.SemaphoreType.DMA,
        ],
        compiler_params=pltpu.CompilerParams(
            collective_id=collective_id, has_side_effects=True
        ),
        cost_estimate=pl.CostEstimate(flops=0, bytes_accessed=70_000_000, transcendentals=0),
    )(x)


def project_kernel(joined, rows_ref, weight_ref, out_ref, *rest):
    each = rows_ref.shape[0]
    rows = rows_ref[...]
    floats = rows.astype(F32)
    squares = floats * floats
    coarse = squares.astype(BF16)
    fine = (squares - coarse.astype(F32)).astype(BF16)
    ones = jnp.ones((8, rows.shape[1]), BF16)
    dims = (((1,), (1,)), ((), ()))
    sums = lax.dot_general(ones, coarse, dims, preferred_element_type=F32)
    sums += lax.dot_general(ones, fine, dims, preferred_element_type=F32)
    for half in range(2):
        for pair in range(KVH // 2):
            first = (half * KVH + pair * 2) * HD
            raw = jnp.dot(
                rows, weight_ref[:, first : first + 2 * HD], preferred_element_type=F32
            ).astype(out_ref.dtype)
            for i in range(2):
                out_ref[pair * 2 + i, 0, :each, half * HD : (half + 1) * HD] = raw[
                    :, i * HD : (i + 1) * HD
                ]
    for h in range(KVH):
        if joined:
            out_ref[h, 0, each:, :] = sums[:, : 2 * HD]
            for part in range(1, each // (2 * HD)):
                out_ref[h, 0, each + part : each + part + 1, :] = sums[
                    :1, part * 2 * HD : (part + 1) * 2 * HD
                ]
        else:
            rest[0][h, 0] = sums


def project(rows, weight, parts, joined):
    count, depth = rows.shape
    each = count // parts
    if joined:
        shapes = [jax.ShapeDtypeStruct((KVH, parts, each + 8, 2 * HD), F32)]
    else:
        shapes = [
            jax.ShapeDtypeStruct((KVH, parts, each, 2 * HD), BF16),
            jax.ShapeDtypeStruct((KVH, parts, 8, each), F32),
        ]
    outs = pl.pallas_call(
        functools.partial(project_kernel, joined),
        grid=(parts,),
        out_shape=shapes,
        in_specs=[
            pl.BlockSpec((each, depth), lambda p: (p, 0)),
            pl.BlockSpec(weight.shape, lambda p: (0, 0)),
        ],
        out_specs=[
            pl.BlockSpec((KVH, 1) + shape.shape[2:], lambda p: (0, p, 0, 0)) for shape in shapes
        ],
        cost_estimate=pl.CostEstimate(
            flops=2 * count * depth * KVH * 2 * HD,
            bytes_accessed=count * depth * 10,
            transcendentals=0,
        ),
    )(rows, weight)
    return [out.reshape((KVH * parts,) + out.shape[2:]) for out in outs]


def whole_text(total):
    total = total[0]
    each = total.shape[0] - 8
    squares = total[each : each + each // (2 * HD)].reshape(each)
    inverse = lax.rsqrt(squares / D + EPS)
    share = (total[:each] * inverse[:, None]).astype(BF16)
    return lax.all_gather(share, ("ctx",) + SUB, axis=0, tiled=True)


def whole_image(visual, weight, parts):
    pieces, squares = project(visual, weight, parts, False)
    pieces, squares = exchange((pieces, squares), VIS, False, 3)
    total = jnp.sum(pieces.astype(F32), axis=0)
    inverse = lax.rsqrt(jnp.sum(squares[:, 0, :], axis=0) / D + EPS)
    share = (total * inverse[:, None]).astype(BF16)
    (whole,) = exchange((share,), ("ctx",) + SUB, True, 4)
    return whole.reshape(-1, 2 * HD)


def per_device(
    patches,
    vis_gain,
    w_qkv,
    w_out,
    merge_gain,
    w_merge,
    token_dest,
    token_row,
    prompt_text,
    kv_gain,
    w_kv,
    queries,
    resp_kv,
    resp_len,
):
    parts = lax.axis_size("vh") * lax.axis_size("core")
    vis_count = lax.axis_size("vk") * parts
    ctx_count = lax.axis_size("ctx")
    vis_index = flat_index(VIS, tuple(lax.axis_size(name) for name in VIS))
    patch_count = patches.shape[0]
    shard_rows = prompt_text.shape[0]
    local_heads = VHEADS // vis_count

    floats = patches.astype(F32)
    normed = layer_norm(floats, vis_gain).astype(BF16)
    gathered = line_gather(normed, 2, 0).reshape(-1, VD)
    few = w_out.shape[0] // ctx_count
    w_out_all = lax.all_gather(
        lax.dynamic_slice_in_dim(w_out, lax.axis_index("ctx") * few, few, 0),
        ("ctx",) + VIS,
        axis=0,
        tiled=True,
    )

    weight = (w_kv.astype(F32) * kv_gain[:, None]).astype(BF16)
    weight, gathered, w_out_all = lax.optimization_barrier((weight, gathered, w_out_all))
    text_total = lax.psum_scatter(
        project(prompt_text, weight, parts, True)[0], VIS, scatter_dimension=0, tiled=True
    )

    qkv = jnp.dot(gathered, w_qkv, preferred_element_type=F32).astype(BF16)
    heads = vision_attention(qkv, local_heads)
    heads = heads.reshape(-1, vis_count, patch_count).transpose(1, 0, 2)
    (returned,) = exchange((heads,), VIS, False, 1)
    returned = returned.reshape(vis_count, ctx_count, few, patch_count).transpose(1, 0, 2, 3)
    projected = jnp.einsum(
        "dp,de->pe", returned.reshape(VD, patch_count), w_out_all, preferred_element_type=F32
    )
    mixed = floats + projected
    merged = layer_norm(mixed, merge_gain).astype(BF16).reshape(patch_count // 4, MD)
    merged = line_gather(merged, 2, 2).reshape(-1, MD)
    merged, text_total = lax.optimization_barrier((merged, text_total))
    text_kv = whole_text(text_total)
    visual = jnp.dot(merged, w_merge, preferred_element_type=F32).astype(BF16)
    image_kv = whole_image(visual, weight, parts)

    flat = (token_dest * shard_rows + token_row).reshape(-1)
    positions = jnp.arange(ctx_count * shard_rows, dtype=jnp.int32)
    taken = jnp.any(positions[:, None] == flat[None, :], axis=1)

    width = KVH * HD
    group = QH // KVH
    mine = QH // vis_count
    resp_rows = queries.shape[0]
    scale = 1.0 / math.sqrt(HD)
    query = lax.dynamic_slice_in_dim(queries, vis_index * mine * HD, mine * HD, 1)
    query = query.reshape(resp_rows, mine, HD).transpose(1, 0, 2).reshape(mine * resp_rows, HD)
    kv_head = (vis_index * mine) // group
    own_keys = lax.dynamic_slice_in_dim(resp_kv, kv_head * HD, HD, 1)
    own_values = lax.dynamic_slice_in_dim(resp_kv, width + kv_head * HD, HD, 1)
    early_keys = jnp.concatenate([text_kv[:, :HD], own_keys], axis=0)
    early_values = jnp.concatenate([text_kv[:, HD:], own_values], axis=0)
    query_positions = jnp.arange(resp_rows, dtype=jnp.int32)
    causal = query_positions[None, :] <= query_positions[:, None]
    visible = jnp.concatenate(
        [jnp.broadcast_to(~taken[None, :], (resp_rows, taken.shape[0])), causal], axis=1
    )
    visible = jnp.broadcast_to(visible[None], (mine,) + visible.shape).reshape(
        mine * resp_rows, -1
    )

    def scores_of(keys):
        return jnp.einsum("qd,kd->qk", query, keys, preferred_element_type=F32) * scale

    scores = jnp.where(visible, scores_of(early_keys), -1e30)
    early_high = jnp.max(scores, axis=1, keepdims=True)
    expo = jnp.where(visible, jnp.exp(scores - early_high), 0.0)
    early_sum = jnp.sum(expo, axis=1, keepdims=True)
    early_mix = jnp.dot(expo.astype(BF16), early_values, preferred_element_type=F32)

    late_scores = scores_of(image_kv[:, :HD])
    high = jnp.maximum(early_high, jnp.max(late_scores, axis=1, keepdims=True))
    late = jnp.exp(late_scores - high)
    fade = jnp.exp(early_high - high)
    summed = early_sum * fade + jnp.sum(late, axis=1, keepdims=True)
    mix = early_mix * fade + jnp.dot(
        late.astype(BF16), image_kv[:, HD:], preferred_element_type=F32
    )
    live = jnp.tile(query_positions < resp_len[0], mine)[:, None]
    result = jnp.where(live, mix / summed, 0.0).astype(BF16)
    result = result.reshape(mine, resp_rows, HD).transpose(1, 0, 2)
    whole = line_gather(result.reshape(resp_rows, mine * HD), 2, 5)
    return whole.transpose(1, 0, 2).reshape(resp_rows, QH * HD)


def solution(mesh):
    ctx_count, vis_count = mesh.shape["ctx"], mesh.shape["vis"]
    parts = vis_count // KVH
    shape = (ctx_count, vis_count // parts, parts // 2, 2)
    fine = Mesh(mesh.devices.reshape(shape), ("ctx",) + VIS)
    return jax.shard_map(
        per_device,
        mesh=fine,
        in_specs=(
            P(("ctx",) + VIS, None),
            P(),
            P(None, VIS),
            P(VIS, None),
            P(),
            P(None, VIS),
            P(),
            P(),
            P("ctx", VIS),
            P(VIS),
            P(VIS, None),
            P("ctx", None),
            P("ctx", None),
            P("ctx"),
        ),
        out_specs=P("ctx", None),
        check_vma=False,
    )
```

```python
import functools
import math

import jax
import jax.numpy as jnp
from jax import lax
from jax.experimental import pallas as pl
from jax.experimental.pallas import tpu as pltpu
from jax.sharding import Mesh, PartitionSpec as P

VD = 1280
VHEADS = 16
D = 8192
HD = 128
QH = 32
KVH = 4
VHD = 80
MD = 5120


EPS = 1e-06
VIS = ("vk", "vh", "core")
SUB = ("vh", "core")
MESH = pl.DeviceIdType.MESH
VMEM = pl.BlockSpec(memory_space=pltpu.VMEM)
F32 = jnp.float32
BF16 = jnp.bfloat16


def layer_norm(values, gain):
    center = values - jnp.mean(values, axis=-1, keepdims=True)
    spread = jnp.mean(center * center, axis=-1, keepdims=True)
    return center * lax.rsqrt(spread + EPS) * gain


def vision_attention(qkv, local_heads):
    scale = 1.0 / math.sqrt(VHD)
    outs = []
    for h in range(local_heads):
        base = h * 3 * VHD
        query = qkv[:, base : base + VHD]
        keys = qkv[:, base + VHD : base + 2 * VHD]
        values = qkv[:, base + 2 * VHD : base + 3 * VHD]
        scores = jnp.einsum("qd,kd->qk", query, keys, preferred_element_type=F32) * scale
        expo = jnp.exp(scores - jnp.max(scores, axis=1, keepdims=True))
        summed = jnp.sum(expo, axis=1, keepdims=True)
        mixed = jnp.einsum("qk,kd->dq", expo.astype(BF16), values, preferred_element_type=F32)
        outs.append((mixed / summed.reshape(1, -1)).astype(BF16))
    return jnp.concatenate(outs, axis=0)


def flat_index(names, sizes):
    index = 0
    for name, size in zip(names, sizes):
        index = index * size + lax.axis_index(name)
    return index


def coordinates(index, names, sizes):
    place = {}
    for name, size in reversed(list(zip(names, sizes))):
        place[name] = index % size
        index = index // size
    return place


def exchange_kernel(names, sizes, spread, count, *refs):
    xs, outs = refs[:count], refs[count : 2 * count]
    send_sem, recv_sem, local_sem = refs[2 * count :]
    total = math.prod(sizes)
    me = flat_index(names, sizes)
    barrier = pltpu.get_barrier_semaphore()
    for step in range(1, total):
        pl.semaphore_signal(
            barrier,
            inc=1,
            device_id=coordinates((me + step) % total, names, sizes),
            device_id_type=MESH,
        )
    pl.semaphore_wait(barrier, total - 1)
    copies = []
    for step in range(1, total):
        target = (me + step) % total
        for i in range(count):
            copy = pltpu.make_async_remote_copy(
                src_ref=xs[i] if spread else xs[i].at[target],
                dst_ref=outs[i].at[me],
                send_sem=send_sem.at[i, step],
                recv_sem=recv_sem.at[i, step],
                device_id=coordinates(target, names, sizes),
                device_id_type=MESH,
            )
            copy.start()
            copies.append(copy)
    for i in range(count):
        own = pltpu.make_async_copy(
            xs[i] if spread else xs[i].at[me], outs[i].at[me], local_sem.at[i]
        )
        own.start()
        copies.append(own)
    for copy in copies:
        copy.wait()


def exchange(xs, names, spread, collective_id):
    sizes = tuple(lax.axis_size(name) for name in names)
    total, count = math.prod(sizes), len(xs)
    shapes = [((total,) + x.shape) if spread else x.shape for x in xs]
    return pl.pallas_call(
        functools.partial(exchange_kernel, names, sizes, spread, count),
        out_shape=[jax.ShapeDtypeStruct(sh, x.dtype) for sh, x in zip(shapes, xs)],
        in_specs=[VMEM] * count,
        out_specs=[VMEM] * count,
        scratch_shapes=[
            pltpu.SemaphoreType.DMA((count, total)),
            pltpu.SemaphoreType.DMA((count, total)),
            pltpu.SemaphoreType.DMA((count,)),
        ],
        compiler_params=pltpu.CompilerParams(
            collective_id=collective_id, has_side_effects=True
        ),
        cost_estimate=pl.CostEstimate(flops=0, bytes_accessed=30_000_000, transcendentals=0),
    )(*xs)


def line_kernel(sizes, chunks, x_ref, out_ref, send_sem, recv_sem, share_send, share_recv, local_sem):
    chips = sizes[0] * sizes[1]
    core = lax.axis_index("core")
    chip = lax.axis_index("vk") * sizes[1] + lax.axis_index("vh")
    rows = x_ref.shape[0] // chunks

    def at(where, which):
        return {"vk": where // sizes[1], "vh": where % sizes[1], "core": which}

    def neighbour(direction):
        return chip + 1 if direction == 0 else chip - 1

    def has(direction):
        return chip < chips - 1 if direction == 0 else chip > 0

    barrier = pltpu.get_barrier_semaphore()
    pl.semaphore_signal(barrier, inc=1, device_id=at(chip, 1 - core), device_id_type=MESH)
    for direction in range(2):
        @pl.when(has(direction))
        def _():
            pl.semaphore_signal(
                barrier, inc=1, device_id=at(neighbour(direction), core), device_id_type=MESH
            )
    pl.semaphore_wait(barrier, 1 + jnp.where(has(0), 1, 0) + jnp.where(has(1), 1, 0))

    def slot(origin, which, piece):
        return out_ref.at[origin * 2 + which, pl.ds(piece * rows, rows)]

    def source(origin, piece, hop):
        return x_ref.at[pl.ds(piece * rows, rows)] if hop == 0 else slot(origin, core, piece)

    def origin_of(direction, hop):
        return chip - hop if direction == 0 else chip + hop

    def exists(direction, hop):
        return chip >= hop if direction == 0 else chip + hop < chips

    def pass_on(direction, hop, piece):
        origin = origin_of(direction, hop)
        return pltpu.make_async_remote_copy(
            src_ref=source(origin, piece, hop),
            dst_ref=slot(origin, core, piece),
            send_sem=send_sem.at[direction, hop, piece],
            recv_sem=recv_sem.at[direction, hop, piece],
            device_id=at(neighbour(direction), core),
            device_id_type=MESH,
        )

    def arrival(direction, hop, piece):
        origin = origin_of(direction, hop)
        return pltpu.make_async_remote_copy(
            src_ref=slot(origin, core, piece),
            dst_ref=slot(origin, core, piece),
            send_sem=send_sem.at[direction, hop - 1, piece],
            recv_sem=recv_sem.at[direction, hop - 1, piece],
            device_id=at(chip, 1 - core),
            device_id_type=MESH,
        )

    def share(origin, piece, hop):
        return pltpu.make_async_remote_copy(
            src_ref=source(origin, piece, hop),
            dst_ref=slot(origin, core, piece),
            send_sem=share_send.at[origin, piece],
            recv_sem=share_recv.at[origin, piece],
            device_id=at(chip, 1 - core),
            device_id_type=MESH,
        )

    for piece in range(chunks):
        for direction in range(2):
            @pl.when(has(direction))
            def _():
                pass_on(direction, 0, piece).start()
    own = pltpu.make_async_copy(x_ref, out_ref.at[chip * 2 + core], local_sem)
    own.start()
    for piece in range(chunks):
        share(chip, piece, 0).start()
    for hop in range(1, chips):
        for piece in range(chunks):
            for direction in range(2):
                @pl.when(exists(direction, hop))
                def _():
                    arrival(direction, hop, piece).wait_recv()
                    if hop < chips - 1:
                        @pl.when(has(direction))
                        def _():
                            pass_on(direction, hop, piece).start()
                    share(origin_of(direction, hop), piece, hop).start()
    own.wait()
    for piece in range(chunks):
        share(chip, piece, 0).wait_send()
        for direction in range(2):
            for hop in range(chips):
                if hop < chips - 1:
                    @pl.when(jnp.logical_and(exists(direction, hop), has(direction)))
                    def _():
                        pass_on(direction, hop, piece).wait_send()
                if hop > 0:
                    @pl.when(exists(direction, hop))
                    def _():
                        share(origin_of(direction, hop), piece, hop).wait_send()
        for origin in range(chips):
            pltpu.make_async_remote_copy(
                src_ref=slot(origin, 1 - core, piece),
                dst_ref=slot(origin, 1 - core, piece),
                send_sem=share_send.at[origin, piece],
                recv_sem=share_recv.at[origin, piece],
                device_id=at(chip, 1 - core),
                device_id_type=MESH,
            ).wait_recv()


def line_gather(x, chunks, collective_id):
    sizes = tuple(lax.axis_size(name) for name in VIS)
    chips = sizes[0] * sizes[1]
    return pl.pallas_call(
        functools.partial(line_kernel, sizes, chunks),
        out_shape=jax.ShapeDtypeStruct((2 * chips,) + x.shape, x.dtype),
        in_specs=[VMEM],
        out_specs=VMEM,
        scratch_shapes=[
            pltpu.SemaphoreType.DMA((2, chips, chunks)),
            pltpu.SemaphoreType.DMA((2, chips, chunks)),
            pltpu.SemaphoreType.DMA((chips, chunks)),
            pltpu.SemaphoreType.DMA((chips, chunks)),
            pltpu.SemaphoreType.DMA,
        ],
        compiler_params=pltpu.CompilerParams(
            collective_id=collective_id, has_side_effects=True
        ),
        cost_estimate=pl.CostEstimate(flops=0, bytes_accessed=70_000_000, transcendentals=0),
    )(x)


def project_kernel(joined, rows_ref, weight_ref, out_ref, *rest):
    each = rows_ref.shape[0]
    rows = rows_ref[...]
    floats = rows.astype(F32)
    squares = floats * floats
    coarse = squares.astype(BF16)
    fine = (squares - coarse.astype(F32)).astype(BF16)
    ones = jnp.ones((8, rows.shape[1]), BF16)
    dims = (((1,), (1,)), ((), ()))
    sums = lax.dot_general(ones, coarse, dims, preferred_element_type=F32)
    sums += lax.dot_general(ones, fine, dims, preferred_element_type=F32)
    for half in range(2):
        for pair in range(KVH // 2):
            first = (half * KVH + pair * 2) * HD
            raw = jnp.dot(
                rows, weight_ref[:, first : first + 2 * HD], preferred_element_type=F32
            ).astype(out_ref.dtype)
            for i in range(2):
                out_ref[pair * 2 + i, 0, :each, half * HD : (half + 1) * HD] = raw[
                    :, i * HD : (i + 1) * HD
                ]
    for h in range(KVH):
        if joined:
            out_ref[h, 0, each:, :] = sums[:, : 2 * HD]
            for part in range(1, each // (2 * HD)):
                out_ref[h, 0, each + part : each + part + 1, :] = sums[
                    :1, part * 2 * HD : (part + 1) * 2 * HD
                ]
        else:
            rest[0][h, 0] = sums


def project(rows, weight, parts, joined):
    count, depth = rows.shape
    each = count // parts
    if joined:
        shapes = [jax.ShapeDtypeStruct((KVH, parts, each + 8, 2 * HD), F32)]
    else:
        shapes = [
            jax.ShapeDtypeStruct((KVH, parts, each, 2 * HD), BF16),
            jax.ShapeDtypeStruct((KVH, parts, 8, each), F32),
        ]
    outs = pl.pallas_call(
        functools.partial(project_kernel, joined),
        grid=(parts,),
        out_shape=shapes,
        in_specs=[
            pl.BlockSpec((each, depth), lambda p: (p, 0)),
            pl.BlockSpec(weight.shape, lambda p: (0, 0)),
        ],
        out_specs=[
            pl.BlockSpec((KVH, 1) + shape.shape[2:], lambda p: (0, p, 0, 0)) for shape in shapes
        ],
        cost_estimate=pl.CostEstimate(
            flops=2 * count * depth * KVH * 2 * HD,
            bytes_accessed=count * depth * 10,
            transcendentals=0,
        ),
    )(rows, weight)
    return [out.reshape((KVH * parts,) + out.shape[2:]) for out in outs]


def whole_text(total):
    total = total[0]
    each = total.shape[0] - 8
    squares = total[each : each + each // (2 * HD)].reshape(each)
    inverse = lax.rsqrt(squares / D + EPS)
    share = (total[:each] * inverse[:, None]).astype(BF16)
    return lax.all_gather(share, ("ctx",) + SUB, axis=0, tiled=True)


def whole_image(visual, weight, parts):
    pieces, squares = project(visual, weight, parts, False)
    pieces, squares = exchange((pieces, squares), VIS, False, 3)
    total = jnp.sum(pieces.astype(F32), axis=0)
    inverse = lax.rsqrt(jnp.sum(squares[:, 0, :], axis=0) / D + EPS)
    share = (total * inverse[:, None]).astype(BF16)
    (whole,) = exchange((share,), ("ctx",) + SUB, True, 4)
    return whole.reshape(-1, 2 * HD)


def per_device(
    patches,
    vis_gain,
    w_qkv,
    w_out,
    merge_gain,
    w_merge,
    token_dest,
    token_row,
    prompt_text,
    kv_gain,
    w_kv,
    queries,
    resp_kv,
    resp_len,
):
    parts = lax.axis_size("vh") * lax.axis_size("core")
    vis_count = lax.axis_size("vk") * parts
    ctx_count = lax.axis_size("ctx")
    vis_index = flat_index(VIS, tuple(lax.axis_size(name) for name in VIS))
    patch_count = patches.shape[0]
    shard_rows = prompt_text.shape[0]
    local_heads = VHEADS // vis_count

    floats = patches.astype(F32)
    normed = layer_norm(floats, vis_gain).astype(BF16)
    gathered = line_gather(normed, 2, 0).reshape(-1, VD)
    few = w_out.shape[0] // ctx_count
    w_out_all = lax.all_gather(
        lax.dynamic_slice_in_dim(w_out, lax.axis_index("ctx") * few, few, 0),
        ("ctx",) + VIS,
        axis=0,
        tiled=True,
    )

    weight = (w_kv.astype(F32) * kv_gain[:, None]).astype(BF16)

    qkv = jnp.dot(gathered, w_qkv, preferred_element_type=F32).astype(BF16)
    heads = vision_attention(qkv, local_heads)
    heads = heads.reshape(-1, vis_count, patch_count).transpose(1, 0, 2)
    (returned,) = exchange((heads,), VIS, False, 1)
    weight, returned, w_out_all = lax.optimization_barrier((weight, returned, w_out_all))
    text_total = lax.psum_scatter(
        project(prompt_text, weight, parts, True)[0], VIS, scatter_dimension=0, tiled=True
    )
    returned = returned.reshape(vis_count, ctx_count, few, patch_count).transpose(1, 0, 2, 3)
    projected = jnp.einsum(
        "dp,de->pe", returned.reshape(VD, patch_count), w_out_all, preferred_element_type=F32
    )
    mixed = floats + projected
    merged = layer_norm(mixed, merge_gain).astype(BF16).reshape(patch_count // 4, MD)
    merged = line_gather(merged, 2, 2).reshape(-1, MD)
    visual = jnp.dot(merged, w_merge, preferred_element_type=F32).astype(BF16)
    visual, text_total = lax.optimization_barrier((visual, text_total))
    text_kv = whole_text(text_total)
    image_kv = whole_image(visual, weight, parts)

    flat = (token_dest * shard_rows + token_row).reshape(-1)
    positions = jnp.arange(ctx_count * shard_rows, dtype=jnp.int32)
    taken = jnp.any(positions[:, None] == flat[None, :], axis=1)

    width = KVH * HD
    group = QH // KVH
    mine = QH // vis_count
    resp_rows = queries.shape[0]
    scale = 1.0 / math.sqrt(HD)
    query = lax.dynamic_slice_in_dim(queries, vis_index * mine * HD, mine * HD, 1)
    query = query.reshape(resp_rows, mine, HD).transpose(1, 0, 2).reshape(mine * resp_rows, HD)
    kv_head = (vis_index * mine) // group
    own_keys = lax.dynamic_slice_in_dim(resp_kv, kv_head * HD, HD, 1)
    own_values = lax.dynamic_slice_in_dim(resp_kv, width + kv_head * HD, HD, 1)
    early_keys = jnp.concatenate([text_kv[:, :HD], own_keys], axis=0)
    early_values = jnp.concatenate([text_kv[:, HD:], own_values], axis=0)
    query_positions = jnp.arange(resp_rows, dtype=jnp.int32)
    causal = query_positions[None, :] <= query_positions[:, None]
    visible = jnp.concatenate(
        [jnp.broadcast_to(~taken[None, :], (resp_rows, taken.shape[0])), causal], axis=1
    )
    visible = jnp.broadcast_to(visible[None], (mine,) + visible.shape).reshape(
        mine * resp_rows, -1
    )

    def scores_of(keys):
        return jnp.einsum("qd,kd->qk", query, keys, preferred_element_type=F32) * scale

    scores = jnp.where(visible, scores_of(early_keys), -1e30)
    early_high = jnp.max(scores, axis=1, keepdims=True)
    expo = jnp.where(visible, jnp.exp(scores - early_high), 0.0)
    early_sum = jnp.sum(expo, axis=1, keepdims=True)
    early_mix = jnp.dot(expo.astype(BF16), early_values, preferred_element_type=F32)

    late_scores = scores_of(image_kv[:, :HD])
    high = jnp.maximum(early_high, jnp.max(late_scores, axis=1, keepdims=True))
    late = jnp.exp(late_scores - high)
    fade = jnp.exp(early_high - high)
    summed = early_sum * fade + jnp.sum(late, axis=1, keepdims=True)
    mix = early_mix * fade + jnp.dot(
        late.astype(BF16), image_kv[:, HD:], preferred_element_type=F32
    )
    live = jnp.tile(query_positions < resp_len[0], mine)[:, None]
    result = jnp.where(live, mix / summed, 0.0).astype(BF16)
    result = result.reshape(mine, resp_rows, HD).transpose(1, 0, 2)
    whole = line_gather(result.reshape(resp_rows, mine * HD), 2, 5)
    return whole.transpose(1, 0, 2).reshape(resp_rows, QH * HD)


def solution(mesh):
    ctx_count, vis_count = mesh.shape["ctx"], mesh.shape["vis"]
    parts = vis_count // KVH
    shape = (ctx_count, vis_count // parts, parts // 2, 2)
    fine = Mesh(mesh.devices.reshape(shape), ("ctx",) + VIS)
    return jax.shard_map(
        per_device,
        mesh=fine,
        in_specs=(
            P(("ctx",) + VIS, None),
            P(),
            P(None, VIS),
            P(VIS, None),
            P(),
            P(None, VIS),
            P(),
            P(),
            P("ctx", VIS),
            P(VIS),
            P(VIS, None),
            P("ctx", None),
            P("ctx", None),
            P("ctx"),
        ),
        out_specs=P("ctx", None),
        check_vma=False,
    )
```
